1024 devices in a mesh: hi: 64 (over y_hi, z, core), lo: 16 (over y_lo, x).
Axes of the slice: x: 8, y: 8 (y_hi: 4, y_lo: 2; y = y_hi * 2 + y_lo), z: 8, core: 2. Of those that a mesh axis runs over, the one named last changes fastest.
Arguments:
- amplitudes: float32 [2, 33554432], P(None, ('hi', 'lo')), may hold values from -6 to 6
- gate_mats: float32 [5, 2, 128, 128], replicated, may hold values from -0.375 to 0.375
- dev_gate: float32 [2, 2, 2], replicated, may hold values from -3 to 3
- qubit_order: int32 [15], replicated, may hold values from 0 to 14, each once
Outputs:
- final_state: float32 [2, 33554432], P(None, ('hi', 'lo'))
The draws below stay inside these ranges and needn't reach their ends.
Inputs may be any that keep to these rules, and one draw needn't show every extreme that they name: `qubit_order`: each of the 15 positions appears exactly once.
All inputs are finite; a program needn't handle non-finite values.
Results may differ from the reference program's by a relative error of at most 0.000068.
Values sent between devices are 32-bit elements; how exact they have to be, the bound alone decides.
A program may use at most 128 MiB of HBM per device.

```python
import jax
import jax.numpy as jnp
from jax import lax

LOCAL_BITS = 15
GATES = 5
AMP_DEV = 32768
GATE_DIM = 128
AMPS = 33554432
N_HI = 64
N_LO = 16


def shard_levels(stream_key, extent, split, low, largest):
    gain = 1.0
    for axis_at, shards_of in split:
        draws = jax.random.uniform(jax.random.fold_in(jax.random.fold_in(stream_key, 6), axis_at), (shards_of,), jnp.float32, low / len(split), largest / len(split))
        gain = gain * jnp.repeat(jnp.exp(draws), extent[axis_at] // shards_of).reshape((-1,) + (1,) * (len(extent) - 1 - axis_at))
    return gain


def bell_draw(rng, shape, scale, reach, shards=(), kind=jnp.bfloat16):
    factor_of = shard_levels(rng, shape, shards, -0.22, 0.18) if shards else 1.0
    result = jax.random.normal(rng, shape, jnp.float32) * scale * factor_of
    return jnp.minimum(jnp.maximum(result, -reach), reach).astype(kind)


def setup_inputs(seed: int = 0) -> dict:
    splits = jax.random.split(jax.random.key(seed), 5)
    amplitudes = bell_draw(splits[0], (2, AMPS), 1.0, 6.0, ((1, 1024),), jnp.float32)
    gate_mats = bell_draw(splits[1], (GATES, 2, GATE_DIM, GATE_DIM), (2 * GATE_DIM) ** -0.5, 0.375, (), jnp.float32)
    dev_gate = bell_draw(splits[2], (2, 2, 2), 4 ** -0.5, 3.0, (), jnp.float32)
    qubit_order = jax.random.permutation(splits[3], LOCAL_BITS).astype(jnp.int32)
    return {"amplitudes": amplitudes, "gate_mats": gate_mats, "dev_gate": dev_gate, "qubit_order": qubit_order}


def apply_matrix(matrix, values, pattern):
    mix_rr = jnp.einsum(pattern, matrix[0], values[0], precision=lax.Precision.HIGHEST)
    mix_ii = jnp.einsum(pattern, matrix[1], values[1], precision=lax.Precision.HIGHEST)
    mix_ri = jnp.einsum(pattern, matrix[0], values[1], precision=lax.Precision.HIGHEST)
    mix_ir = jnp.einsum(pattern, matrix[1], values[0], precision=lax.Precision.HIGHEST)
    return jnp.stack([mix_rr - mix_ii, mix_ri + mix_ir])


def low_gate(matrix, values):
    gate_width = matrix.shape[-1]
    shaped = values.reshape(2, -1, gate_width)
    return apply_matrix(matrix, shaped, "ab,mb->ma").reshape(values.shape)


def high_gate(matrix, values):
    gate_width = matrix.shape[-1]
    shaped = values.reshape(2, -1, gate_width, AMP_DEV // gate_width)
    return apply_matrix(matrix, shaped, "ab,cbm->cam").reshape(values.shape)


def mix_pair(dev_gate, row_index, lower_pair, upper_pair):
    coef_0r = dev_gate[0, row_index, 0]
    coef_0i = dev_gate[1, row_index, 0]
    coef_1r = dev_gate[0, row_index, 1]
    coef_1i = dev_gate[1, row_index, 1]
    real_part = (coef_0r * lower_pair[0] - coef_0i * lower_pair[1]) + (coef_1r * upper_pair[0] - coef_1i * upper_pair[1])
    imag_part = (coef_0r * lower_pair[1] + coef_0i * lower_pair[0]) + (coef_1r * upper_pair[1] + coef_1i * upper_pair[0])
    return jnp.stack([real_part, imag_part])


def source_table(qubit_order, amp_count):
    positions = jnp.arange(amp_count, dtype=jnp.int32)
    source = jnp.zeros((amp_count,), jnp.int32)
    for position in range(qubit_order.shape[0]):
        source = source + jnp.left_shift(jnp.right_shift(positions, position) & 1, qubit_order[position])
    return source


def reference(amplitudes, gate_mats, dev_gate, qubit_order):
    halves = amplitudes.reshape(2, 2, -1)
    lower_pair = halves[:, 0]
    upper_pair = halves[:, 1]
    state_now = jnp.stack([mix_pair(dev_gate, 0, lower_pair, upper_pair), mix_pair(dev_gate, 1, lower_pair, upper_pair)], axis=1).reshape(2, -1)
    state_now = high_gate(gate_mats[0], state_now)
    state_now = low_gate(gate_mats[1], state_now)
    source = source_table(qubit_order, AMP_DEV)
    state_now = jnp.take(state_now.reshape(2, N_HI * N_LO, AMP_DEV), source, axis=2).reshape(2, -1)
    state_now = state_now.reshape(2, N_HI, N_LO, N_LO, AMP_DEV // N_LO).swapaxes(2, 3).reshape(2, -1)
    state_now = high_gate(gate_mats[2], state_now)
    state_now = low_gate(gate_mats[3], state_now)
    return high_gate(gate_mats[4], state_now)
```

```python
import functools

import jax
import jax.numpy as jnp
from jax import lax
from jax.experimental import pallas as pl
from jax.experimental.pallas import tpu as pltpu
from jax.sharding import PartitionSpec as P

MESH = pl.DeviceIdType.MESH
F32, BF16, I32 = jnp.float32, jnp.bfloat16, jnp.int32
W = 128
NT = (((1,), (1,)), ((), ()))
NN = (((1,), (0,)), ((), ()))


def split(x):
    high = x.astype(BF16)
    return high, (x - high.astype(F32)).astype(BF16)


def dot(a, b, dims=NN):
    return lax.dot_general(a, b, dims, preferred_element_type=F32)


def dot3(a, b, dims=NN):
    return dot(a[0], b[0], dims) + (dot(a[1], b[0], dims) + dot(a[0], b[1], dims))


def real_form(re, im):
    return tuple(
        jnp.concatenate([jnp.concatenate([r, -i], 1), jnp.concatenate([i, r], 1)], 0)
        for r, i in zip(re, im)
    )


def one_hot(size, moves):
    row = lax.broadcasted_iota(I32, (size, size), 0)
    col = lax.broadcasted_iota(I32, (size, size), 1)
    source = jnp.zeros((size, size), I32)
    for from_bit, to_bit in moves:
        source = source | (((row >> from_bit) & 1) << to_bit)
    return jnp.where(source == col, 1.0, 0.0).astype(BF16)


def plan(order, table):
    new_lanes = jnp.int32(0)
    for k in range(7):
        new_lanes = new_lanes | (jnp.int32(1) << order[k])
    goes_lane = [(new_lanes >> s) & 1 for s in range(15)]
    count = goes_lane[8]
    for s in range(9, 15):
        count = count + goes_lane[s]
    row_slot, leave, stay = [], jnp.int32(0), count
    for s in range(8, 15):
        out = goes_lane[s]
        row_slot.append(jnp.where(out == 1, leave, stay))
        table[s] = jnp.where(out == 1, leave, 7 + 6 - stay)
        leave, stay = leave + out, stay + 1 - out
    table[7] = jnp.where(goes_lane[7] == 1, 6, 7 + 7)
    lane_slot, leave, stay = [], jnp.int32(0), count
    for s in range(7):
        out = 1 - goes_lane[s]
        place = jnp.where(leave < count, leave, 6)
        lane_slot.append(jnp.where(out == 1, place, stay))
        table[s] = jnp.where(out == 1, jnp.where(leave < count, 7 + 6 - leave, 7 + 7), stay)
        leave, stay = leave + out, stay + 1 - out
    flags = [jnp.where(count > i, 1, 0) for i in range(7)]
    place_of = [table[order[k]] for k in range(15)]
    return row_slot, lane_slot, flags, goes_lane[7], place_of


def swap_outer(z, lane, bit, stride, flag):
    rows = z.shape[0]
    shift = 1 << bit
    one = (lane >> bit) & 1
    z = z.reshape(rows // (2 * stride), 2, stride, W)
    low, high = z[:, 0], z[:, 1]
    flat = (rows // 2, W)
    low, high = low.reshape(flat), high.reshape(flat)
    up = pltpu.roll(high, shift, 1)
    down = pltpu.roll(low, W - shift, 1)
    new_low = jnp.where(one * flag == 1, up, low)
    new_high = jnp.where((1 - one) * flag == 1, down, high)
    part = (rows // (2 * stride), 1, stride, W)
    return jnp.concatenate([new_low.reshape(part), new_high.reshape(part)], 1).reshape(rows, W)


def swap_inner(z, lane, sub, bit, level, flag):
    rows = z.shape[0]
    shift, step = 1 << bit, 1 << level
    lane_one = (lane >> bit) & 1
    sub_one = (sub >> level) & 1
    moved = jnp.where(sub_one == 1, pltpu.roll(z, shift, 1), pltpu.roll(z, W - shift, 1))
    moved = moved.reshape(rows // 8, 8, W)
    if step == 4:
        other = pltpu.roll(moved, 4, 1).reshape(rows, W)
    else:
        fore = pltpu.roll(moved, 8 - step, 1).reshape(rows, W)
        back = pltpu.roll(moved, step, 1).reshape(rows, W)
        other = jnp.where(sub_one == 0, fore, back)
    return jnp.where((lane_one ^ sub_one) * flag == 1, other, z)


def kernel(n_hi, n_lo, order, dev, state, gates, out, table, send, recv, send_sem, recv_sem, own_sem):
    hi, lo = lax.axis_index("hi"), lax.axis_index("lo")
    half = n_hi // 2
    other = lax.rem(hi + half, n_hi)
    peers = [(other, lax.rem(lo + k, n_lo), 1) for k in range(n_lo)]
    peers += [(hi, lax.rem(lo + k, n_lo), 0) for k in range(1, n_lo)]

    barrier = pltpu.get_barrier_semaphore()
    for to_hi, to_lo, _ in peers:
        pl.semaphore_signal(barrier, inc=1, device_id=(to_hi, to_lo), device_id_type=MESH)

    row_slot, lane_slot, flags, flag_b, place_of = plan(order, table)

    def parts(g):
        return split(gates[g, 0]), split(gates[g, 1])

    def permuted(g, moves):
        re, im = parts(g)
        stacked = jnp.concatenate([re[0], re[1], im[0], im[1]], 1)
        moved = dot(one_hot(W, moves), stacked).astype(BF16)
        return real_form((moved[:, :W], moved[:, W : 2 * W]), (moved[:, 2 * W : 3 * W], moved[:, 3 * W :]))

    first = permuted(0, [(6 - row_slot[u], u) for u in range(7)])
    second = permuted(1, [(lane_slot[u], u) for u in range(7)])

    blocks = [[state[pl.ds(2 * b + c, W, stride=4), :] for b in range(2)] for c in range(2)]
    now = jnp.concatenate([jnp.concatenate(blocks[c], 1) for c in range(2)], 0)
    now = dot3(first, split(now))
    now = jnp.concatenate(
        [jnp.concatenate([now[:W, b * W : b * W + W], now[W:, b * W : b * W + W]], 1) for b in range(2)], 0
    )
    now = dot3(split(now), second, NT)
    now = jnp.concatenate([now[:, :W], now[:, W:]], 0)
    lane = lax.broadcasted_iota(I32, (1, W), 1)
    sub = lax.broadcasted_iota(I32, (4 * W, W), 0) & 7
    for i in range(4):
        now = swap_outer(now, lane, i, 64 >> i, flags[i])
    now = swap_outer(now, lane, 6, 128, flag_b)
    for i in range(4, 7):
        now = swap_inner(now, lane, sub, i, 6 - i, flags[i])
    index_of = {7: 3, 8: 0, 9: 1, 10: 2, 11: 4, 12: 5, 13: 6, 14: 7}
    rows = one_hot(2 * W, [(index_of[k], place_of[k] - 7) for k in range(7, 15)])
    now = split(jnp.concatenate([now[: 2 * W], now[2 * W :]], 1))
    now = dot(rows, now[0]) + dot(rows, now[1])
    for c in range(2):
        send[:, c] = now[:, c * W : c * W + W].reshape(n_lo, 16, W)

    pl.semaphore_wait(barrier, len(peers))
    copies = []
    for k, (to_hi, to_lo, which) in enumerate(peers):
        copies.append(
            pltpu.make_async_remote_copy(
                src_ref=send.at[to_lo],
                dst_ref=recv.at[which, lo],
                send_sem=send_sem.at[k],
                recv_sem=recv_sem.at[k],
                device_id=(to_hi, to_lo),
                device_id_type=MESH,
            )
        )
        copies[-1].start()
    own = pltpu.make_async_copy(send.at[lo], recv.at[0, lo], own_sem)
    own.start()

    re, im = parts(3)
    lanes = one_hot(W, [(k, place_of[k]) for k in range(7)])
    moved = dot(jnp.concatenate([re[0], re[1], im[0], im[1]], 0), lanes).astype(BF16)
    third = real_form((moved[:W], moved[W : 2 * W]), (moved[2 * W : 3 * W], moved[3 * W :]))
    fourth = real_form(*parts(4))
    joined = dot3(fourth, split(jnp.concatenate([gates[2, 0], gates[2, 1]], 0)))
    joined = real_form(split(joined[:W]), split(joined[W:]))
    t = hi // half
    s = 1 - t
    vr, vi, wr, wi = dev[0, t, t], dev[1, t, t], dev[0, t, s], dev[1, t, s]

    own.wait()
    for copy in copies:
        copy.wait()

    pr, pi = (recv[0, :, c].reshape(2 * W, W) for c in range(2))
    qr, qi = (recv[1, :, c].reshape(2 * W, W) for c in range(2))
    mix_r = (vr * pr - vi * pi) + (wr * qr - wi * qi)
    mix_i = (vr * pi + vi * pr) + (wr * qi + wi * qr)
    now = dot3(split(jnp.concatenate([mix_r, mix_i], 1)), third, NT)
    now = now.reshape(n_lo, 2, 8, 2 * W)
    now = [now[:, b].reshape(W, 2 * W) for b in range(2)]
    now = jnp.concatenate(
        [jnp.concatenate([now[b][:, c * W : c * W + W] for b in range(2)], 1) for c in range(2)], 0
    )
    now = dot3(joined, split(now))
    for c in range(2):
        for b in range(2):
            out[pl.ds(2 * b + c, W, stride=4), :] = now[c * W : c * W + W, b * W : b * W + W]


def on_device(n_hi, n_lo, amplitudes, gate_mats, dev_gate, qubit_order):
    amps = amplitudes.shape[1]
    state = amplitudes.reshape(2, amps // W, W).transpose(1, 0, 2).reshape(-1, W)
    n_copies = 2 * n_lo - 1
    done = pl.pallas_call(
        functools.partial(kernel, n_hi, n_lo),
        name="window",
        out_shape=jax.ShapeDtypeStruct(state.shape, F32),
        in_specs=[pl.BlockSpec(memory_space=pltpu.SMEM)] * 2 + [pl.BlockSpec(memory_space=pltpu.VMEM)] * 2,
        out_specs=pl.BlockSpec(memory_space=pltpu.VMEM),
        scratch_shapes=[
            pltpu.SMEM((16,), I32),
            pltpu.VMEM((n_lo, 2, 16, W), F32),
            pltpu.VMEM((2, n_lo, 2, 16, W), F32),
            pltpu.SemaphoreType.DMA((n_copies,)),
            pltpu.SemaphoreType.DMA((n_copies,)),
            pltpu.SemaphoreType.DMA,
        ],
        compiler_params=pltpu.CompilerParams(collective_id=0, has_side_effects=True),
    )(qubit_order, dev_gate, state, gate_mats)
    return done.reshape(amps // W, 2, W).transpose(1, 0, 2).reshape(2, amps)


def solution(mesh):
    return jax.shard_map(
        functools.partial(on_device, mesh.shape["hi"], mesh.shape["lo"]),
        mesh=mesh,
        in_specs=(P(None, ("hi", "lo")), P(), P(), P()),
        out_specs=P(None, ("hi", "lo")),
        check_vma=False,
    )
```

```python
import functools

import jax
import jax.numpy as jnp
from jax import lax
from jax.experimental import pallas as pl
from jax.experimental.pallas import tpu as pltpu
from jax.sharding import PartitionSpec as P

MESH = pl.DeviceIdType.MESH
F32, BF16, I32 = jnp.float32, jnp.bfloat16, jnp.int32
W = 128
NT = (((1,), (1,)), ((), ()))
NN = (((1,), (0,)), ((), ()))


def split(x):
    high = x.astype(BF16)
    return high, (x - high.astype(F32)).astype(BF16)


def dot(a, b, dims=NN):
    return lax.dot_general(a, b, dims, preferred_element_type=F32)


def dot3(a, b, dims=NN):
    return dot(a[0], b[0], dims) + (dot(a[1], b[0], dims) + dot(a[0], b[1], dims))


def real_form(re, im):
    return tuple(
        jnp.concatenate([jnp.concatenate([r, -i], 1), jnp.concatenate([i, r], 1)], 0)
        for r, i in zip(re, im)
    )


def one_hot(size, moves):
    row = lax.broadcasted_iota(I32, (size, size), 0)
    col = lax.broadcasted_iota(I32, (size, size), 1)
    source = jnp.zeros((size, size), I32)
    for from_bit, to_bit in moves:
        source = source | (((row >> from_bit) & 1) << to_bit)
    return jnp.where(source == col, 1.0, 0.0).astype(BF16)


def plan(order, table):
    new_lanes = jnp.int32(0)
    for k in range(7):
        new_lanes = new_lanes | (jnp.int32(1) << order[k])
    goes_lane = [(new_lanes >> s) & 1 for s in range(15)]
    count = goes_lane[8]
    for s in range(9, 15):
        count = count + goes_lane[s]
    row_slot, leave, stay = [], jnp.int32(0), count
    for s in range(8, 15):
        out = goes_lane[s]
        row_slot.append(jnp.where(out == 1, leave, stay))
        table[s] = jnp.where(out == 1, leave, 7 + 6 - stay)
        leave, stay = leave + out, stay + 1 - out
    table[7] = jnp.where(goes_lane[7] == 1, 6, 7 + 7)
    lane_slot, leave, stay = [], jnp.int32(0), count
    for s in range(7):
        out = 1 - goes_lane[s]
        place = jnp.where(leave < count, leave, 6)
        lane_slot.append(jnp.where(out == 1, place, stay))
        table[s] = jnp.where(out == 1, jnp.where(leave < count, 7 + 6 - leave, 7 + 7), stay)
        leave, stay = leave + out, stay + 1 - out
    flags = [jnp.where(count > i, 1, 0) for i in range(7)]
    place_of = [table[order[k]] for k in range(15)]
    return row_slot, lane_slot, flags, goes_lane[7], place_of


def swap_outer(z, lane, bit, stride, flag):
    rows = z.shape[0]
    shift = 1 << bit
    one = (lane >> bit) & 1
    z = z.reshape(rows // (2 * stride), 2, stride, W)
    low, high = z[:, 0], z[:, 1]
    flat = (rows // 2, W)
    low, high = low.reshape(flat), high.reshape(flat)
    up = pltpu.roll(high, shift, 1)
    down = pltpu.roll(low, W - shift, 1)
    new_low = jnp.where(one * flag == 1, up, low)
    new_high = jnp.where((1 - one) * flag == 1, down, high)
    part = (rows // (2 * stride), 1, stride, W)
    return jnp.concatenate([new_low.reshape(part), new_high.reshape(part)], 1).reshape(rows, W)


def swap_inner(z, lane, sub, bit, level, flag):
    rows = z.shape[0]
    shift, step = 1 << bit, 1 << level
    lane_one = (lane >> bit) & 1
    sub_one = (sub >> level) & 1
    moved = jnp.where(sub_one == 1, pltpu.roll(z, shift, 1), pltpu.roll(z, W - shift, 1))
    moved = moved.reshape(rows // 8, 8, W)
    if step == 4:
        other = pltpu.roll(moved, 4, 1).reshape(rows, W)
    else:
        fore = pltpu.roll(moved, 8 - step, 1).reshape(rows, W)
        back = pltpu.roll(moved, step, 1).reshape(rows, W)
        other = jnp.where(sub_one == 0, fore, back)
    return jnp.where((lane_one ^ sub_one) * flag == 1, other, z)


def kernel(n_hi, n_lo, order_hbm, dev_hbm, state_hbm, gates_hbm, out, table, order, dev, state, gates, send, row, fin,
           load_sem, own_sem, x_send, x_recv, y_send, y_recv, ready):
    hi, lo = lax.axis_index("hi"), lax.axis_index("lo")
    half, n_x = n_hi // 2, n_lo // 2
    mine, base = hi // half, hi % half
    side = base // (half // 2)
    flip, x = lo // n_x, lo % n_x

    def rank(w, yl, at):
        y = 2 * (side + 2 * w) + yl
        hops = at + y - (at // 4) * (2 * at - 8) - (y // 4) * (2 * y - 8)
        return hops * 64 + w * n_lo + yl * n_x + at

    def member(w, yl, at):
        return w, yl, at, rank(w, yl, at) - rank(mine, flip, x)

    def to(peer):
        return {"device_id": (base + peer[0] * half, peer[1] * n_x + peer[2]), "device_id_type": MESH}

    def number(peer):
        return peer[0] * n_lo + peer[1] * n_x + peer[2]

    row_peers = [member(mine, flip, (x + d) % n_x) for d in (1, 7, 2, 6, 3, 5, 4)]
    y_peers = [member(mine, 1 - flip, x), member(1 - mine, flip, x), member(1 - mine, 1 - flip, x)]
    peers = row_peers + y_peers
    wanted = [1 - flip, flip, 1 - flip]

    barrier = pltpu.get_barrier_semaphore()
    for peer in peers:
        pl.semaphore_signal(barrier, inc=1, **to(peer))

    small = [pltpu.make_async_copy(order_hbm, order, load_sem.at[6]), pltpu.make_async_copy(dev_hbm, dev, load_sem.at[7])]
    small[0].start()
    loads = [pltpu.make_async_copy(state_hbm, state, load_sem.at[0])]
    loads += [pltpu.make_async_copy(gates_hbm.at[g], gates.at[g], load_sem.at[1 + g]) for g in range(5)]
    for load in loads:
        load.start()
    small[1].start()

    small[0].wait()
    row_slot, lane_slot, flags, flag_b, place_of = plan(order, table)

    def parts(g):
        return split(gates[g, 0]), split(gates[g, 1])

    def permuted(g, moves):
        re, im = parts(g)
        stacked = jnp.concatenate([re[0], re[1], im[0], im[1]], 1)
        moved = dot(one_hot(W, moves), stacked).astype(BF16)
        return real_form((moved[:, :W], moved[:, W : 2 * W]), (moved[:, 2 * W : 3 * W], moved[:, 3 * W :]))

    loads[1].wait()
    first = permuted(0, [(6 - row_slot[u], u) for u in range(7)])
    loads[2].wait()
    second = permuted(1, [(lane_slot[u], u) for u in range(7)])

    loads[0].wait()
    blocks = [[state[pl.ds(2 * b + c, W, stride=4), :] for b in range(2)] for c in range(2)]
    now = jnp.concatenate([jnp.concatenate(blocks[c], 1) for c in range(2)], 0)
    now = dot3(first, split(now))
    now = jnp.concatenate(
        [jnp.concatenate([now[:W, b * W : b * W + W], now[W:, b * W : b * W + W]], 1) for b in range(2)], 0
    )
    now = dot3(split(now), second, NT)
    now = jnp.concatenate([now[:, :W], now[:, W:]], 0)
    lane = lax.broadcasted_iota(I32, (1, W), 1)
    sub = lax.broadcasted_iota(I32, (4 * W, W), 0) & 7
    for i in range(4):
        now = swap_outer(now, lane, i, 64 >> i, flags[i])
    now = swap_outer(now, lane, 6, 128, flag_b)
    for i in range(4, 7):
        now = swap_inner(now, lane, sub, i, 6 - i, flags[i])
    index_of = {7: 3, 8: 0, 9: 1, 10: 2, 11: 5, 12: 6, 13: 7, 14: 4}
    rows = one_hot(2 * W, [(index_of[k], place_of[k] - 7) for k in range(7, 15)])
    now = split(jnp.concatenate([now[: 2 * W], now[2 * W :]], 1))
    now = dot(rows, now[0]) + dot(rows, now[1])
    for c in range(2):
        send[:, :, c] = now[:, c * W : c * W + W].reshape(n_x, 2, 16, W)

    pl.semaphore_wait(barrier, 10)

    def along_x(peer):
        return pltpu.make_async_remote_copy(
            src_ref=send.at[peer[2]], dst_ref=row.at[x], send_sem=x_send.at[peer[2]], recv_sem=x_recv.at[x], **to(peer)
        )

    def from_x(peer):
        return pltpu.make_async_remote_copy(
            src_ref=send.at[peer[2]], dst_ref=row.at[peer[2]], send_sem=x_send.at[peer[2]], recv_sem=x_recv.at[peer[2]], **to(peer)
        )

    def along_y(j, at, source):
        return pltpu.make_async_remote_copy(
            src_ref=source.at[at, wanted[j]], dst_ref=fin.at[j, at], send_sem=y_send.at[j, at], recv_sem=y_recv.at[j, at], **to(y_peers[j])
        )

    for peer in row_peers:
        along_x(peer).start()
    own = pltpu.make_async_copy(send.at[x], row.at[x], own_sem)
    own.start()
    for j in (1, 2, 0):
        along_y(j, x, send).start()
    for peer in row_peers:
        from_x(peer).wait_recv()
        for j in (1, 2, 0):
            along_y(j, peer[2], row).start()

    for load in loads[3:]:
        load.wait()
    re, im = parts(3)
    lanes = one_hot(W, [(k, place_of[k]) for k in range(7)])
    moved = dot(jnp.concatenate([re[0], re[1], im[0], im[1]], 0), lanes).astype(BF16)
    third = real_form((moved[:W], moved[W : 2 * W]), (moved[2 * W : 3 * W], moved[3 * W :]))
    fourth = real_form(*parts(4))
    joined = dot3(fourth, split(jnp.concatenate([gates[2, 0], gates[2, 1]], 0)))
    joined = jnp.where(lane * 0 + flip == 1, pltpu.roll(joined, W // 2, 1), joined)
    joined = real_form(split(joined[:W]), split(joined[W:]))
    s = 1 - mine
    small[1].wait()
    vr, vi, wr, wi = dev[0, mine, mine], dev[1, mine, mine], dev[0, mine, s], dev[1, mine, s]

    own.wait()
    for peer in row_peers:
        from_x(peer).wait_send()
    for j in range(3):
        for at in range(n_x):
            along_y(j, at, row).wait()

    def halves(near, far, c):
        return jnp.concatenate([near[c], far[c]], 0)

    def load_half(ref):
        return [ref[:, c].reshape(W, W) for c in range(2)]

    p = load_half(row.at[:, flip]), load_half(fin.at[0])
    q = load_half(fin.at[1]), load_half(fin.at[2])
    pr, pi = halves(*p, 0), halves(*p, 1)
    qr, qi = halves(*q, 0), halves(*q, 1)
    mix_r = (vr * pr - vi * pi) + (wr * qr - wi * qi)
    mix_i = (vr * pi + vi * pr) + (wr * qi + wi * qr)
    now = dot3(split(jnp.concatenate([mix_r, mix_i], 1)), third, NT)
    now = now.reshape(n_lo, 2, 8, 2 * W)
    now = [now[:, b].reshape(W, 2 * W) for b in range(2)]
    now = jnp.concatenate(
        [jnp.concatenate([now[b][:, c * W : c * W + W] for b in range(2)], 1) for c in range(2)], 0
    )
    now = dot3(joined, split(now))
    for c in range(2):
        for b in range(2):
            out[pl.ds(2 * b + c, W, stride=4), :] = now[c * W : c * W + W, b * W : b * W + W]


def on_device(n_hi, n_lo, amplitudes, gate_mats, dev_gate, qubit_order):
    amps = amplitudes.shape[1]
    n_x = n_lo // 2
    state = amplitudes.reshape(2, amps // W, W).transpose(1, 0, 2).reshape(-1, W)
    dma = pltpu.SemaphoreType.DMA
    done = pl.pallas_call(
        functools.partial(kernel, n_hi, n_lo),
        name="window",
        out_shape=pltpu.VMEM(state.shape, F32),
        in_specs=[pl.BlockSpec(memory_space=pl.ANY)] * 4,
        out_specs=pl.BlockSpec(memory_space=pltpu.VMEM),
        scratch_shapes=[
            pltpu.SMEM((16,), I32),
            pltpu.SMEM(qubit_order.shape, I32),
            pltpu.SMEM(dev_gate.shape, F32),
            pltpu.VMEM(state.shape, F32),
            pltpu.VMEM(gate_mats.shape, F32),
            pltpu.VMEM((n_x, 2, 2, 16, W), F32),
            pltpu.VMEM((n_x, 2, 2, 16, W), F32),
            pltpu.VMEM((3, n_x, 2, 16, W), F32),
            dma((8,)),
            dma,
            dma((n_x,)),
            dma((n_x,)),
            dma((3, n_x)),
            dma((3, n_x)),
            pltpu.SemaphoreType.REGULAR((2 * n_lo,)),
        ],
        compiler_params=pltpu.CompilerParams(collective_id=0, has_side_effects=True),
    )(qubit_order, dev_gate, state, gate_mats)
    return done.reshape(amps // W, 2, W).transpose(1, 0, 2).reshape(2, amps)


def solution(mesh):
    return jax.shard_map(
        functools.partial(on_device, mesh.shape["hi"], mesh.shape["lo"]),
        mesh=mesh,
        in_specs=(P(None, ("hi", "lo")), P(), P(), P()),
        out_specs=P(None, ("hi", "lo")),
        check_vma=False,
    )
```

```python
import functools

import jax
import jax.numpy as jnp
from jax import lax
from jax.experimental import pallas as pl
from jax.experimental.pallas import tpu as pltpu
from jax.sharding import PartitionSpec as P

MESH = pl.DeviceIdType.MESH
F32, BF16, I32 = jnp.float32, jnp.bfloat16, jnp.int32
W = 128
NT = (((1,), (1,)), ((), ()))
NN = (((1,), (0,)), ((), ()))


def split(x):
    high = x.astype(BF16)
    return high, (x - high.astype(F32)).astype(BF16)


def dot(a, b, dims=NN):
    return lax.dot_general(a, b, dims, preferred_element_type=F32)


def dot3(a, b, dims=NN):
    return dot(a[0], b[0], dims) + (dot(a[1], b[0], dims) + dot(a[0], b[1], dims))


def real_form(re, im):
    return tuple(
        jnp.concatenate([jnp.concatenate([r, -i], 1), jnp.concatenate([i, r], 1)], 0)
        for r, i in zip(re, im)
    )


def one_hot(size, moves):
    row = lax.broadcasted_iota(I32, (size, size), 0)
    col = lax.broadcasted_iota(I32, (size, size), 1)
    source = jnp.zeros((size, size), I32)
    for from_bit, to_bit in moves:
        source = source | (((row >> from_bit) & 1) << to_bit)
    return jnp.where(source == col, 1.0, 0.0).astype(BF16)


def plan(order, table):
    new_lanes = jnp.int32(0)
    for k in range(7):
        new_lanes = new_lanes | (jnp.int32(1) << order[k])
    goes_lane = [(new_lanes >> s) & 1 for s in range(15)]
    count = goes_lane[8]
    for s in range(9, 15):
        count = count + goes_lane[s]
    row_slot, leave, stay = [], jnp.int32(0), count
    for s in range(8, 15):
        out = goes_lane[s]
        row_slot.append(jnp.where(out == 1, leave, stay))
        table[s] = jnp.where(out == 1, leave, 7 + 6 - stay)
        leave, stay = leave + out, stay + 1 - out
    table[7] = jnp.where(goes_lane[7] == 1, 6, 7 + 7)
    lane_slot, leave, stay = [], jnp.int32(0), count
    for s in range(7):
        out = 1 - goes_lane[s]
        place = jnp.where(leave < count, leave, 6)
        lane_slot.append(jnp.where(out == 1, place, stay))
        table[s] = jnp.where(out == 1, jnp.where(leave < count, 7 + 6 - leave, 7 + 7), stay)
        leave, stay = leave + out, stay + 1 - out
    flags = [jnp.where(count > i, 1, 0) for i in range(7)]
    place_of = [table[order[k]] for k in range(15)]
    return row_slot, lane_slot, flags, goes_lane[7], place_of


def swap_outer(z, lane, bit, stride, flag):
    rows = z.shape[0]
    shift = 1 << bit
    one = (lane >> bit) & 1
    z = z.reshape(rows // (2 * stride), 2, stride, W)
    low, high = z[:, 0], z[:, 1]
    flat = (rows // 2, W)
    low, high = low.reshape(flat), high.reshape(flat)
    up = pltpu.roll(high, shift, 1)
    down = pltpu.roll(low, W - shift, 1)
    new_low = jnp.where(one * flag == 1, up, low)
    new_high = jnp.where((1 - one) * flag == 1, down, high)
    part = (rows // (2 * stride), 1, stride, W)
    return jnp.concatenate([new_low.reshape(part), new_high.reshape(part)], 1).reshape(rows, W)


def swap_inner(z, lane, sub, bit, level, flag):
    rows = z.shape[0]
    shift, step = 1 << bit, 1 << level
    lane_one = (lane >> bit) & 1
    sub_one = (sub >> level) & 1
    moved = jnp.where(sub_one == 1, pltpu.roll(z, shift, 1), pltpu.roll(z, W - shift, 1))
    moved = moved.reshape(rows // 8, 8, W)
    if step == 4:
        other = pltpu.roll(moved, 4, 1).reshape(rows, W)
    else:
        fore = pltpu.roll(moved, 8 - step, 1).reshape(rows, W)
        back = pltpu.roll(moved, step, 1).reshape(rows, W)
        other = jnp.where(sub_one == 0, fore, back)
    return jnp.where((lane_one ^ sub_one) * flag == 1, other, z)


def kernel(n_hi, n_lo, order_hbm, dev_hbm, state_hbm, gates_hbm, out, table, order, dev, state, gates, send, stage, relay, row, fin,
           load_sem, x_send, x_recv, y_send, y_recv, ready):
    hi, lo = lax.axis_index("hi"), lax.axis_index("lo")
    half, n_x = n_hi // 2, n_lo // 2
    mine, base = hi // half, hi % half
    side = base // (half // 2)
    flip, x = lo // n_x, lo % n_x

    def is_first(w, yl, at):
        return lax.convert_element_type(base + w * half + yl + at == 0, I32)

    def rank(w, yl, at):
        y = 2 * (side + 2 * w) + yl
        hops = at + y - (at // 4) * (2 * at - 8) - (y // 4) * (2 * y - 8)
        return hops * 64 + w * n_lo + yl * n_x + at + is_first(w, yl, at) * 1024

    def member(w, yl, at):
        return w, yl, at, rank(w, yl, at) - rank(mine, flip, x), is_first(w, yl, at)

    def to(peer):
        return {"device_id": (base + peer[0] * half, peer[1] * n_x + peer[2]), "device_id_type": MESH}

    def number(peer):
        return peer[0] * n_lo + peer[1] * n_x + peer[2]

    row_peers = [member(mine, flip, (x + d) % n_x) for d in (1, 7, 2, 6, 3, 5, 4)]
    special = lax.convert_element_type(base == 0, I32)

    def x_first(n, start, end):
        at_start = special * lax.convert_element_type(start == 0, I32)
        at_end = special * lax.convert_element_type(end == 0, I32)
        return at_start + (1 - at_start) * (1 - at_end) * int(n < 6)

    outward = [x_first(n, x, peer[2]) for n, peer in enumerate(row_peers)]
    inward = [x_first(n, peer[2], x) for n, peer in enumerate(row_peers)]
    y_peers = [member(mine, 1 - flip, x), member(1 - mine, flip, x), member(1 - mine, 1 - flip, x)]
    peers = row_peers + y_peers
    wanted = [1 - flip, flip, 1 - flip]

    barrier = pltpu.get_barrier_semaphore()
    for peer in peers:
        @pl.when(peer[3] > 0)
        def _():
            pl.semaphore_signal(barrier, inc=1, **to(peer))

    known = jnp.int32(0)
    for peer in peers:
        known = known + lax.convert_element_type(peer[3] < 0, I32)

    def greet():
        @pl.when(known > 0)
        def _():
            pl.semaphore_wait(barrier, known)
        for peer in peers:
            @pl.when(peer[3] < 0)
            def _():
                pl.semaphore_signal(ready.at[number((mine, flip, x))], inc=1, **to(peer))

    slow = lax.convert_element_type((x == 6) | (2 * (side + 2 * mine) + flip == 6), I32)

    small = [pltpu.make_async_copy(order_hbm, order, load_sem.at[6]), pltpu.make_async_copy(dev_hbm, dev, load_sem.at[7])]
    small[0].start()
    loads = [pltpu.make_async_copy(state_hbm, state, load_sem.at[0])]
    loads += [pltpu.make_async_copy(gates_hbm.at[g], gates.at[g], load_sem.at[1 + g]) for g in range(5)]
    for load in loads:
        load.start()
    small[1].start()

    small[0].wait()
    row_slot, lane_slot, flags, flag_b, place_of = plan(order, table)

    def parts(g):
        return split(gates[g, 0]), split(gates[g, 1])

    def permuted(g, moves):
        re, im = parts(g)
        stacked = jnp.concatenate([re[0], re[1], im[0], im[1]], 1)
        moved = dot(one_hot(W, moves), stacked).astype(BF16)
        return real_form((moved[:, :W], moved[:, W : 2 * W]), (moved[:, 2 * W : 3 * W], moved[:, 3 * W :]))

    loads[1].wait()
    first = permuted(0, [(6 - row_slot[u], u) for u in range(7)])
    loads[2].wait()
    second = permuted(1, [(lane_slot[u], u) for u in range(7)])

    @pl.when(slow == 0)
    def _():
        greet()

    loads[0].wait()
    blocks = [[state[pl.ds(2 * b + c, W, stride=4), :] for b in range(2)] for c in range(2)]
    now = jnp.concatenate([jnp.concatenate(blocks[c], 1) for c in range(2)], 0)
    now = dot3(first, split(now))
    now = jnp.concatenate(
        [jnp.concatenate([now[:W, b * W : b * W + W], now[W:, b * W : b * W + W]], 1) for b in range(2)], 0
    )
    now = dot3(split(now), second, NT)
    now = jnp.concatenate([now[:, :W], now[:, W:]], 0)
    lane = lax.broadcasted_iota(I32, (1, W), 1)
    sub = lax.broadcasted_iota(I32, (4 * W, W), 0) & 7
    for i in range(4):
        now = swap_outer(now, lane, i, 64 >> i, flags[i])
    now = swap_outer(now, lane, 6, 128, flag_b)
    for i in range(4, 7):
        now = swap_inner(now, lane, sub, i, 6 - i, flags[i])
    index_of = {7: 3, 8: 0, 9: 1, 10: 2, 11: 5, 12: 6, 13: 7, 14: 4}
    rows = one_hot(2 * W, [(index_of[k], place_of[k] - 7) for k in range(7, 15)])
    now = split(jnp.concatenate([now[: 2 * W], now[2 * W :]], 1))
    now = dot(rows, now[0]) + dot(rows, now[1])
    for c in range(2):
        send[:, :, c] = now[:, c * W : c * W + W].reshape(n_x, 2, 16, W)

    @pl.when(slow == 1)
    def _():
        greet()

    def along_x(peer, source, target):
        return pltpu.make_async_remote_copy(
            src_ref=source.at[peer[2]], dst_ref=target.at[x], send_sem=x_send.at[peer[2]], recv_sem=x_recv.at[x], **to(peer)
        )

    def from_x(peer, source, target):
        return pltpu.make_async_remote_copy(
            src_ref=source.at[peer[2]], dst_ref=target.at[peer[2]], send_sem=x_send.at[peer[2]], recv_sem=x_recv.at[peer[2]], **to(peer)
        )

    def along_y(j, at, source=send, leg=0):
        return pltpu.make_async_remote_copy(
            src_ref=source.at[at, wanted[j]], dst_ref=fin.at[leg, j, at],
            send_sem=y_send.at[leg, j, at], recv_sem=y_recv.at[leg, j, at], **to(y_peers[j])
        )

    def when(*terms):
        met = terms[0]
        for term in terms[1:]:
            met = met & term
        return pl.when(met)

    def await_ready(peer):
        pl.semaphore_wait(ready.at[number(peer)], 1)

    for peer, out_x in zip(row_peers, outward):
        @when(out_x == 1, peer[3] < 0)
        def _():
            along_x(peer, send, relay).start()
    far_first = list(zip(row_peers, outward))[::-1]

    def open_y(j):
        for peer, out_x in far_first:
            @when(out_x == 0)
            def _():
                along_y(j, peer[2]).start()
        along_y(j, x).start()

    for j in (1, 2, 0):
        @pl.when(y_peers[j][3] < 0)
        def _():
            open_y(j)
    for peer, out_x in zip(row_peers, outward):
        @when(out_x == 1, peer[3] > 0, peer[4] == 0)
        def _():
            await_ready(peer)
            along_x(peer, send, relay).start()
    for j in (0, 2, 1):
        @when(y_peers[j][3] > 0, y_peers[j][4] == 0)
        def _():
            await_ready(y_peers[j])
            open_y(j)

    for load in loads[3:]:
        load.wait()
    re, im = parts(3)
    lanes = one_hot(W, [(k, place_of[k]) for k in range(7)])
    moved = dot(jnp.concatenate([re[0], re[1], im[0], im[1]], 0), lanes).astype(BF16)
    third = real_form((moved[:W], moved[W : 2 * W]), (moved[2 * W : 3 * W], moved[3 * W :]))
    fourth = real_form(*parts(4))
    joined = dot3(fourth, split(jnp.concatenate([gates[2, 0], gates[2, 1]], 0)))
    joined = jnp.where(lane * 0 + flip == 1, pltpu.roll(joined, W // 2, 1), joined)
    joined = real_form(split(joined[:W]), split(joined[W:]))
    s = 1 - mine
    small[1].wait()
    vr, vi, wr, wi = dev[0, mine, mine], dev[1, mine, mine], dev[0, mine, s], dev[1, mine, s]

    for peer, in_x in zip(row_peers, inward):
        @when(in_x == 1, peer[4] == 0)
        def _():
            from_x(peer, send, relay).wait_recv()
            for j in (1, 2, 0):
                along_y(j, peer[2], relay, 1).start()
    for j in range(3):
        @when(y_peers[j][4] == 1)
        def _():
            await_ready(y_peers[j])
            along_y(j, x).start()

    def mix(at, source, leg, target):
        for j in (0, 1, 2):
            along_y(j, at, send, leg).wait_recv()
        pr, pi = (jnp.concatenate([source[at, flip, c], fin[leg, 0, at, c]], 0) for c in range(2))
        qr, qi = (jnp.concatenate([fin[leg, 1, at, c], fin[leg, 2, at, c]], 0) for c in range(2))
        mix_r = (vr * pr - vi * pi) + (wr * qr - wi * qi)
        mix_i = (vr * pi + vi * pr) + (wr * qi + wi * qr)
        done = dot3(split(jnp.concatenate([mix_r, mix_i], 1)), third, NT)
        for y in range(2):
            for c in range(2):
                target[at, y, c] = done[y * 16 : y * 16 + 16, c * W : c * W + W]

    for peer, out_x in far_first:
        @when(out_x == 0)
        def _():
            mix(peer[2], send, 0, stage)

            @pl.when(peer[4] == 0)
            def _():
                @pl.when(peer[3] > 0)
                def _():
                    await_ready(peer)
                along_x(peer, stage, row).start()
    for peer in row_peers:
        @pl.when(peer[4] == 1)
        def _():
            await_ready(peer)
            along_x(peer, stage, row).start()
            from_x(peer, send, relay).wait_recv()
            for j in (1, 2, 0):
                along_y(j, peer[2], relay, 1).start()
    mix(x, send, 0, row)
    for peer, in_x in zip(row_peers, inward):
        @when(in_x == 1)
        def _():
            mix(peer[2], relay, 1, row)
    for peer, in_x in zip(row_peers, inward):
        @when(in_x == 0)
        def _():
            from_x(peer, stage, row).wait_recv()
        from_x(peer, stage, row).wait_send()
    for j in range(3):
        along_y(j, x).wait_send()
        for peer, out_x, in_x in zip(row_peers, outward, inward):
            @when(out_x == 0)
            def _():
                along_y(j, peer[2]).wait_send()
            @when(in_x == 1)
            def _():
                along_y(j, peer[2], relay, 1).wait_send()

    now = []
    for c in range(2):
        part = jnp.concatenate([row[:, y, c].reshape(W, W) for y in range(2)], 0).reshape(n_lo, 2, 8, W)
        now.append(jnp.concatenate([part[:, b].reshape(W, W) for b in range(2)], 1))
    now = dot3(joined, split(jnp.concatenate(now, 0)))
    for c in range(2):
        for b in range(2):
            out[pl.ds(2 * b + c, W, stride=4), :] = now[c * W : c * W + W, b * W : b * W + W]


def on_device(n_hi, n_lo, amplitudes, gate_mats, dev_gate, qubit_order):
    amps = amplitudes.shape[1]
    n_x = n_lo // 2
    state = amplitudes.reshape(2, amps // W, W).transpose(1, 0, 2).reshape(-1, W)
    dma = pltpu.SemaphoreType.DMA
    done = pl.pallas_call(
        functools.partial(kernel, n_hi, n_lo),
        name="window",
        out_shape=pltpu.VMEM(state.shape, F32),
        in_specs=[pl.BlockSpec(memory_space=pl.ANY)] * 4,
        out_specs=pl.BlockSpec(memory_space=pltpu.VMEM),
        scratch_shapes=[
            pltpu.SMEM((16,), I32),
            pltpu.SMEM(qubit_order.shape, I32),
            pltpu.SMEM(dev_gate.shape, F32),
            pltpu.VMEM(state.shape, F32),
            pltpu.VMEM(gate_mats.shape, F32),
            pltpu.VMEM((n_x, 2, 2, 16, W), F32),
            pltpu.VMEM((n_x, 2, 2, 16, W), F32),
            pltpu.VMEM((n_x, 2, 2, 16, W), F32),
            pltpu.VMEM((n_x, 2, 2, 16, W), F32),
            pltpu.VMEM((2, 3, n_x, 2, 16, W), F32),
            dma((8,)),
            dma((n_x,)),
            dma((n_x,)),
            dma((2, 3, n_x)),
            dma((2, 3, n_x)),
            pltpu.SemaphoreType.REGULAR((2 * n_lo,)),
        ],
        compiler_params=pltpu.CompilerParams(collective_id=0, has_side_effects=True),
    )(qubit_order, dev_gate, state, gate_mats)
    return done.reshape(amps // W, 2, W).transpose(1, 0, 2).reshape(2, amps)


def solution(mesh):
    return jax.shard_map(
        functools.partial(on_device, mesh.shape["hi"], mesh.shape["lo"]),
        mesh=mesh,
        in_specs=(P(None, ("hi", "lo")), P(), P(), P()),
        out_specs=P(None, ("hi", "lo")),
        check_vma=False,
    )
```

```python
import functools

import jax
import jax.numpy as jnp
from jax import lax
from jax.experimental import pallas as pl
from jax.experimental.pallas import tpu as pltpu
from jax.sharding import PartitionSpec as P

MESH = pl.DeviceIdType.MESH
F32, BF16, I32 = jnp.float32, jnp.bfloat16, jnp.int32
W = 128
NT = (((1,), (1,)), ((), ()))
NN = (((1,), (0,)), ((), ()))


def split(x):
    high = x.astype(BF16)
    return high, (x - high.astype(F32)).astype(BF16)


def dot(a, b, dims=NN):
    return lax.dot_general(a, b, dims, preferred_element_type=F32)


def dot3(a, b, dims=NN):
    return dot(a[0], b[0], dims) + (dot(a[1], b[0], dims) + dot(a[0], b[1], dims))


def real_form(re, im):
    return tuple(
        jnp.concatenate([jnp.concatenate([r, -i], 1), jnp.concatenate([i, r], 1)], 0)
        for r, i in zip(re, im)
    )


def one_hot(size, moves):
    row = lax.broadcasted_iota(I32, (size, size), 0)
    col = lax.broadcasted_iota(I32, (size, size), 1)
    source = jnp.zeros((size, size), I32)
    for from_bit, to_bit in moves:
        source = source | (((row >> from_bit) & 1) << to_bit)
    return jnp.where(source == col, 1.0, 0.0).astype(BF16)


def plan(order, table):
    new_lanes = jnp.int32(0)
    for k in range(7):
        new_lanes = new_lanes | (jnp.int32(1) << order[k])
    goes_lane = [(new_lanes >> s) & 1 for s in range(15)]
    count = goes_lane[8]
    for s in range(9, 15):
        count = count + goes_lane[s]
    row_slot, leave, stay = [], jnp.int32(0), count
    for s in range(8, 15):
        out = goes_lane[s]
        row_slot.append(jnp.where(out == 1, leave, stay))
        table[s] = jnp.where(out == 1, leave, 7 + 6 - stay)
        leave, stay = leave + out, stay + 1 - out
    table[7] = jnp.where(goes_lane[7] == 1, 6, 7 + 7)
    lane_slot, leave, stay = [], jnp.int32(0), count
    for s in range(7):
        out = 1 - goes_lane[s]
        place = jnp.where(leave < count, leave, 6)
        lane_slot.append(jnp.where(out == 1, place, stay))
        table[s] = jnp.where(out == 1, jnp.where(leave < count, 7 + 6 - leave, 7 + 7), stay)
        leave, stay = leave + out, stay + 1 - out
    flags = [jnp.where(count > i, 1, 0) for i in range(7)]
    place_of = [table[order[k]] for k in range(15)]
    return row_slot, lane_slot, flags, goes_lane[7], place_of


def swap_outer(z, lane, bit, stride, flag):
    rows = z.shape[0]
    shift = 1 << bit
    one = (lane >> bit) & 1
    z = z.reshape(rows // (2 * stride), 2, stride, W)
    low, high = z[:, 0], z[:, 1]
    flat = (rows // 2, W)
    low, high = low.reshape(flat), high.reshape(flat)
    up = pltpu.roll(high, shift, 1)
    down = pltpu.roll(low, W - shift, 1)
    new_low = jnp.where(one * flag == 1, up, low)
    new_high = jnp.where((1 - one) * flag == 1, down, high)
    part = (rows // (2 * stride), 1, stride, W)
    return jnp.concatenate([new_low.reshape(part), new_high.reshape(part)], 1).reshape(rows, W)


def swap_inner(z, lane, sub, bit, level, flag):
    rows = z.shape[0]
    shift, step = 1 << bit, 1 << level
    lane_one = (lane >> bit) & 1
    sub_one = (sub >> level) & 1
    moved = jnp.where(sub_one == 1, pltpu.roll(z, shift, 1), pltpu.roll(z, W - shift, 1))
    moved = moved.reshape(rows // 8, 8, W)
    if step == 4:
        other = pltpu.roll(moved, 4, 1).reshape(rows, W)
    else:
        fore = pltpu.roll(moved, 8 - step, 1).reshape(rows, W)
        back = pltpu.roll(moved, step, 1).reshape(rows, W)
        other = jnp.where(sub_one == 0, fore, back)
    return jnp.where((lane_one ^ sub_one) * flag == 1, other, z)


def kernel(n_hi, n_lo, order_hbm, dev_hbm, state_hbm, gates_hbm, out, table, order, dev, state, gates, send, stage, relay, row, fin,
           load_sem, x_send, x_recv, y_send, y_recv, ready):
    hi, lo = lax.axis_index("hi"), lax.axis_index("lo")
    half, n_x = n_hi // 2, n_lo // 2
    mine, base = hi // half, hi % half
    side = base // (half // 2)
    flip, x = lo // n_x, lo % n_x

    def is_first(w, yl, at):
        return lax.convert_element_type(base + w * half + yl + at == 0, I32)

    def rank(w, yl, at):
        y = 2 * (side + 2 * w) + yl
        hops = at + y - (at // 4) * (2 * at - 8) - (y // 4) * (2 * y - 8)
        return hops * 64 + w * n_lo + yl * n_x + at + is_first(w, yl, at) * 1024

    def member(w, yl, at):
        return w, yl, at, rank(w, yl, at) - rank(mine, flip, x), is_first(w, yl, at)

    def to(peer):
        return {"device_id": (base + peer[0] * half, peer[1] * n_x + peer[2]), "device_id_type": MESH}

    def number(peer):
        return peer[0] * n_lo + peer[1] * n_x + peer[2]

    row_peers = [member(mine, flip, (x + d) % n_x) for d in (1, 7, 2, 6, 3, 5, 4)]
    special = lax.convert_element_type(base == 0, I32)

    def x_first(n, start, end):
        at_start = special * lax.convert_element_type(start == 0, I32)
        at_end = special * lax.convert_element_type(end == 0, I32)
        return at_start + (1 - at_start) * (1 - at_end) * (int(n < 4) + side * int(4 <= n < 6))

    outward = [x_first(n, x, peer[2]) for n, peer in enumerate(row_peers)]
    inward = [x_first(n, peer[2], x) for n, peer in enumerate(row_peers)]
    y_peers = [member(mine, 1 - flip, x), member(1 - mine, flip, x), member(1 - mine, 1 - flip, x)]
    peers = row_peers + y_peers
    wanted = [1 - flip, flip, 1 - flip]

    barrier = pltpu.get_barrier_semaphore()
    small = [pltpu.make_async_copy(order_hbm, order, load_sem.at[6]), pltpu.make_async_copy(dev_hbm, dev, load_sem.at[7])]
    small[0].start()
    loads = [pltpu.make_async_copy(state_hbm, state, load_sem.at[0])]
    loads += [pltpu.make_async_copy(gates_hbm.at[g], gates.at[g], load_sem.at[1 + g]) for g in range(5)]
    for load in loads:
        load.start()
    small[1].start()

    for peer in peers:
        @pl.when(peer[3] > 0)
        def _():
            pl.semaphore_signal(barrier, inc=1, **to(peer))

    known = jnp.int32(0)
    for peer in peers:
        known = known + lax.convert_element_type(peer[3] < 0, I32)

    def greet():
        @pl.when(known > 0)
        def _():
            pl.semaphore_wait(barrier, known)
        for peer in peers:
            @pl.when(peer[3] < 0)
            def _():
                pl.semaphore_signal(ready.at[number((mine, flip, x))], inc=1, **to(peer))

    slow = lax.convert_element_type((x == 6) | (2 * (side + 2 * mine) + flip == 6), I32)

    column, line = x % 4, (2 * (side + 2 * mine) + flip) % 4
    prompt = lax.convert_element_type((column * (x - 1) == 0) & (line * (2 * (side + 2 * mine) + flip - 1) == 0), I32)

    @pl.when(prompt == 1)
    def _():
        greet()

    small[0].wait()
    row_slot, lane_slot, flags, flag_b, place_of = plan(order, table)

    def parts(g):
        return split(gates[g, 0]), split(gates[g, 1])

    def permuted(g, moves):
        re, im = parts(g)
        stacked = jnp.concatenate([re[0], re[1], im[0], im[1]], 1)
        moved = dot(one_hot(W, moves), stacked).astype(BF16)
        return real_form((moved[:, :W], moved[:, W : 2 * W]), (moved[:, 2 * W : 3 * W], moved[:, 3 * W :]))

    loads[1].wait()
    first = permuted(0, [(6 - row_slot[u], u) for u in range(7)])
    loads[2].wait()
    second = permuted(1, [(lane_slot[u], u) for u in range(7)])

    @pl.when(slow + prompt == 0)
    def _():
        greet()

    loads[0].wait()
    blocks = [[state[pl.ds(2 * b + c, W, stride=4), :] for b in range(2)] for c in range(2)]
    now = jnp.concatenate([jnp.concatenate(blocks[c], 1) for c in range(2)], 0)
    now = dot3(first, split(now))
    now = jnp.concatenate(
        [jnp.concatenate([now[:W, b * W : b * W + W], now[W:, b * W : b * W + W]], 1) for b in range(2)], 0
    )
    now = dot3(split(now), second, NT)
    now = jnp.concatenate([now[:, :W], now[:, W:]], 0)
    lane = lax.broadcasted_iota(I32, (1, W), 1)
    sub = lax.broadcasted_iota(I32, (4 * W, W), 0) & 7
    for i in range(4):
        now = swap_outer(now, lane, i, 64 >> i, flags[i])
    now = swap_outer(now, lane, 6, 128, flag_b)
    for i in range(4, 7):
        now = swap_inner(now, lane, sub, i, 6 - i, flags[i])
    index_of = {7: 3, 8: 0, 9: 1, 10: 2, 11: 5, 12: 6, 13: 7, 14: 4}
    rows = one_hot(2 * W, [(index_of[k], place_of[k] - 7) for k in range(7, 15)])
    now = split(jnp.concatenate([now[: 2 * W], now[2 * W :]], 1))
    now = dot(rows, now[0]) + dot(rows, now[1])
    for c in range(2):
        send[:, :, c] = now[:, c * W : c * W + W].reshape(n_x, 2, 16, W)

    @pl.when(slow == 1)
    def _():
        greet()

    def along_x(peer, source, target):
        return pltpu.make_async_remote_copy(
            src_ref=source.at[peer[2]], dst_ref=target.at[x], send_sem=x_send.at[peer[2]], recv_sem=x_recv.at[x], **to(peer)
        )

    def from_x(peer, source, target):
        return pltpu.make_async_remote_copy(
            src_ref=source.at[peer[2]], dst_ref=target.at[peer[2]], send_sem=x_send.at[peer[2]], recv_sem=x_recv.at[peer[2]], **to(peer)
        )

    def along_y(j, at, source=send, leg=0):
        return pltpu.make_async_remote_copy(
            src_ref=source.at[at, wanted[j]], dst_ref=fin.at[leg, j, at],
            send_sem=y_send.at[leg, j, at], recv_sem=y_recv.at[leg, j, at], **to(y_peers[j])
        )

    def when(*terms):
        met = terms[0]
        for term in terms[1:]:
            met = met & term
        return pl.when(met)

    def await_ready(peer):
        pl.semaphore_wait(ready.at[number(peer)], 1)

    for peer, out_x in zip(row_peers, outward):
        @when(out_x == 1, peer[3] < 0)
        def _():
            along_x(peer, send, relay).start()
    far_first = list(zip(row_peers, outward))[::-1]

    def open_y(j):
        for peer, out_x in far_first:
            @when(out_x == 0)
            def _():
                along_y(j, peer[2]).start()
        along_y(j, x).start()

    for j in (1, 2, 0):
        @pl.when(y_peers[j][3] < 0)
        def _():
            open_y(j)
    for load in loads[3:]:
        load.wait()
    re, im = parts(3)
    lanes = one_hot(W, [(k, place_of[k]) for k in range(7)])
    moved = dot(jnp.concatenate([re[0], re[1], im[0], im[1]], 0), lanes).astype(BF16)
    third = real_form((moved[:W], moved[W : 2 * W]), (moved[2 * W : 3 * W], moved[3 * W :]))
    fourth = real_form(*parts(4))
    joined = dot3(fourth, split(jnp.concatenate([gates[2, 0], gates[2, 1]], 0)))
    joined = jnp.where(lane * 0 + flip == 1, pltpu.roll(joined, W // 2, 1), joined)
    joined = real_form(split(joined[:W]), split(joined[W:]))
    s = 1 - mine
    small[1].wait()
    vr, vi, wr, wi = dev[0, mine, mine], dev[1, mine, mine], dev[0, mine, s], dev[1, mine, s]

    def later_x(n, *terms):
        peer, out_x = row_peers[n], outward[n]

        @when(out_x == 1, peer[3] > 0, peer[4] == 0, *terms)
        def _():
            await_ready(peer)
            along_x(peer, send, relay).start()

    def later_y(j):
        @when(y_peers[j][3] > 0, y_peers[j][4] == 0)
        def _():
            await_ready(y_peers[j])
            open_y(j)

    for n in range(2):
        later_x(n, row_peers[n][2] != 6)
    later_y(0)
    for n in range(2, 7):
        later_x(n, row_peers[n][2] != 6)
    later_y(2)
    later_y(1)
    for n in range(7):
        later_x(n, row_peers[n][2] == 6)

    for peer, in_x in zip(row_peers, inward):
        @when(in_x == 1, peer[4] == 0)
        def _():
            from_x(peer, send, relay).wait_recv()
            for j in (1, 2, 0):
                along_y(j, peer[2], relay, 1).start()
    for j in range(3):
        @when(y_peers[j][4] == 1)
        def _():
            await_ready(y_peers[j])
            along_y(j, x).start()

    def mix(at, source, leg, target):
        for j in (0, 1, 2):
            along_y(j, at, send, leg).wait_recv()
        pr, pi = (jnp.concatenate([source[at, flip, c], fin[leg, 0, at, c]], 0) for c in range(2))
        qr, qi = (jnp.concatenate([fin[leg, 1, at, c], fin[leg, 2, at, c]], 0) for c in range(2))
        mix_r = (vr * pr - vi * pi) + (wr * qr - wi * qi)
        mix_i = (vr * pi + vi * pr) + (wr * qi + wi * qr)
        done = dot3(split(jnp.concatenate([mix_r, mix_i], 1)), third, NT)
        for y in range(2):
            for c in range(2):
                target[at, y, c] = done[y * 16 : y * 16 + 16, c * W : c * W + W]

    for peer, out_x in far_first:
        @when(out_x == 0)
        def _():
            mix(peer[2], send, 0, stage)

            @pl.when(peer[4] == 0)
            def _():
                @pl.when(peer[3] > 0)
                def _():
                    await_ready(peer)
                along_x(peer, stage, row).start()
    for peer in row_peers:
        @pl.when(peer[4] == 1)
        def _():
            await_ready(peer)
            along_x(peer, stage, row).start()
            from_x(peer, send, relay).wait_recv()
            for j in (1, 2, 0):
                along_y(j, peer[2], relay, 1).start()
    mix(x, send, 0, row)
    for peer, in_x in zip(row_peers, inward):
        @when(in_x == 1)
        def _():
            mix(peer[2], relay, 1, row)
    for peer, in_x in zip(row_peers, inward):
        @when(in_x == 0)
        def _():
            from_x(peer, stage, row).wait_recv()
        from_x(peer, stage, row).wait_send()
    for j in range(3):
        along_y(j, x).wait_send()
        for peer, out_x, in_x in zip(row_peers, outward, inward):
            @when(out_x == 0)
            def _():
                along_y(j, peer[2]).wait_send()
            @when(in_x == 1)
            def _():
                along_y(j, peer[2], relay, 1).wait_send()

    now = []
    for c in range(2):
        part = jnp.concatenate([row[:, y, c].reshape(W, W) for y in range(2)], 0).reshape(n_lo, 2, 8, W)
        now.append(jnp.concatenate([part[:, b].reshape(W, W) for b in range(2)], 1))
    now = dot3(joined, split(jnp.concatenate(now, 0)))
    for c in range(2):
        for b in range(2):
            out[pl.ds(2 * b + c, W, stride=4), :] = now[c * W : c * W + W, b * W : b * W + W]


def on_device(n_hi, n_lo, amplitudes, gate_mats, dev_gate, qubit_order):
    amps = amplitudes.shape[1]
    n_x = n_lo // 2
    state = amplitudes.reshape(2, amps // W, W).transpose(1, 0, 2).reshape(-1, W)
    dma = pltpu.SemaphoreType.DMA
    done = pl.pallas_call(
        functools.partial(kernel, n_hi, n_lo),
        name="window",
        out_shape=pltpu.VMEM(state.shape, F32),
        in_specs=[pl.BlockSpec(memory_space=pl.ANY)] * 4,
        out_specs=pl.BlockSpec(memory_space=pltpu.VMEM),
        scratch_shapes=[
            pltpu.SMEM((16,), I32),
            pltpu.SMEM(qubit_order.shape, I32),
            pltpu.SMEM(dev_gate.shape, F32),
            pltpu.VMEM(state.shape, F32),
            pltpu.VMEM(gate_mats.shape, F32),
            pltpu.VMEM((n_x, 2, 2, 16, W), F32),
            pltpu.VMEM((n_x, 2, 2, 16, W), F32),
            pltpu.VMEM((n_x, 2, 2, 16, W), F32),
            pltpu.VMEM((n_x, 2, 2, 16, W), F32),
            pltpu.VMEM((2, 3, n_x, 2, 16, W), F32),
            dma((8,)),
            dma((n_x,)),
            dma((n_x,)),
            dma((2, 3, n_x)),
            dma((2, 3, n_x)),
            pltpu.SemaphoreType.REGULAR((2 * n_lo,)),
        ],
        compiler_params=pltpu.CompilerParams(collective_id=0, has_side_effects=True),
    )(qubit_order, dev_gate, state, gate_mats)
    return done.reshape(amps // W, 2, W).transpose(1, 0, 2).reshape(2, amps)


def solution(mesh):
    return jax.shard_map(
        functools.partial(on_device, mesh.shape["hi"], mesh.shape["lo"]),
        mesh=mesh,
        in_specs=(P(None, ("hi", "lo")), P(), P(), P()),
        out_specs=P(None, ("hi", "lo")),
        check_vma=False,
    )
```
